128 devices in a mesh: frame: 8 (over y, core), strip: 16 (over x, z).
Axes of the slice: x: 4, y: 4, z: 4, core: 2. Of those that a mesh axis runs over, the one named last changes fastest.
Arguments:
- tokens: bfloat16 [8, 32, 128, 768], P('frame', 'strip'), may hold values from -6 to 6
- timestep: int32 [1], replicated, may hold values from 0 to 999
- col_order: int32 [128], replicated, may hold values from 0 to 127, each once
- row_order: int32 [32], replicated, may hold values from 0 to 31, each once
- w_time: bfloat16 [256, 3072], replicated, may hold values from -0.375 to 0.375
- w_in: bfloat16 [2, 768, 3328], replicated, may hold values from -0.21875 to 0.21875
- w_dt: bfloat16 [2, 768, 24], replicated, may hold values from -0.21875 to 0.21875
- conv_w: float32 [2, 4, 1792], replicated, may hold values from -0.5 to 0.5
- conv_b: float32 [2, 1792], replicated, may hold values from -3 to 3
- dt_bias: float32 [2, 24], replicated, may hold values from -1 to 0.5
- a_log: float32 [2, 24], replicated
- d_skip: float32 [2, 24], replicated, may hold values from 0.5 to 2
- out_gain: float32 [2, 1536], replicated, may hold values from 0.1 to 1.9
- w_out: bfloat16 [2, 1536, 768], replicated, may hold values from -0.15625 to 0.15625
Outputs:
- denoised: bfloat16 [8, 32, 128, 768], P('frame', None, 'strip')
The draws below stay inside these ranges and needn't reach their ends.
Inputs may be any that keep to these rules, and one draw needn't show every extreme that they name: `col_order`: a permutation. `row_order`: a permutation.
All inputs are finite; a program needn't handle non-finite values.
Results may differ from the reference program's by a relative error of at most 0.015.
Values may be sent and summed in bfloat16 or wider, within the bound.
A program may use at most 256 MiB of HBM per device.

```python
import math
import jax
import jax.numpy as jnp
from jax import lax

D = 768
HEADS = 24
HDIM = 64
STATE = 128
CONV = 4
GROUP = 256
FREQ = 256
INNER = 1536
CONVW = 1792
FRAMES = 8
HH = 32
WW = 128


def draw_a_log(key, part):
    sequence_length = FRAMES * HH * WW
    coin_draw = jax.random.randint(jax.random.fold_in(key, 11), (2, HEADS), 0, 8)
    quick_heads = coin_draw < 4
    fast_log = jax.random.uniform(jax.random.fold_in(key, 12), (2, HEADS), jnp.float32, math.log(0.03), math.log(0.15))
    slow_log = jax.random.uniform(jax.random.fold_in(key, 13), (2, HEADS), jnp.float32, math.log(0.3), math.log(3.0))
    slow_log = slow_log - math.log(sequence_length)
    return jnp.where(quick_heads, fast_log, slow_log).astype(jnp.float32)


def draw_tokens(key, part):
    noise = jax.random.normal(jax.random.fold_in(key, 21), (FRAMES, HH, WW, D), jnp.float32)
    direction = jax.random.normal(jax.random.fold_in(key, 22), (D,), jnp.float32)
    frame_level = jax.random.uniform(jax.random.fold_in(key, 23), (FRAMES,), jnp.float32, -1.4, 1.4)
    row_level = jax.random.uniform(jax.random.fold_in(key, 24), (HH,), jnp.float32, -1.4, 1.4)
    col_level = jax.random.uniform(jax.random.fold_in(key, 25), (WW,), jnp.float32, -1.4, 1.4)
    level = frame_level[:, None, None] + row_level[None, :, None] + col_level[None, None, :]
    values = noise + level[..., None] * direction
    return jnp.clip(values, -6.0, 6.0).astype(jnp.bfloat16)


def bell_draw(rng, extent, deviation, bound, kind=jnp.bfloat16):
    return jnp.clip(deviation * jax.random.normal(rng, extent, jnp.float32), -bound, bound).astype(kind)


def setup_inputs(seed: int = 0) -> dict:
    key_of = jax.random.split(jax.random.key(seed), 15)
    return {
        "tokens": draw_tokens(jax.random.fold_in(key_of[14], 71), 0),
        "timestep": jax.random.randint(key_of[1], (1,), 0, 1000).astype(jnp.int32),
        "col_order": jax.random.permutation(key_of[2], WW).astype(jnp.int32),
        "row_order": jax.random.permutation(key_of[3], HH).astype(jnp.int32),
        "w_time": bell_draw(key_of[4], (FREQ, 4 * D), FREQ ** -0.5, 0.375),
        "w_in": bell_draw(key_of[5], (2, D, INNER + CONVW), D ** -0.5, 0.21875),
        "w_dt": bell_draw(key_of[6], (2, D, HEADS), D ** -0.5, 0.21875),
        "conv_w": jnp.clip(jax.random.uniform(key_of[7], (2, CONV, CONVW), jnp.float32, -0.5, 0.5), -0.5, 0.5),
        "conv_b": bell_draw(key_of[8], (2, CONVW), 0.5, 3.0, jnp.float32),
        "dt_bias": jnp.clip(jax.random.uniform(key_of[9], (2, HEADS), jnp.float32, -1.0, 0.5), -1.0, 0.5),
        "a_log": draw_a_log(jax.random.fold_in(key_of[14], 71), 0),
        "d_skip": jnp.clip(jax.random.uniform(key_of[11], (2, HEADS), jnp.float32, 0.5, 2.0), 0.5, 2.0),
        "out_gain": jnp.clip(1.0 + 0.18 * jax.random.normal(key_of[12], (2, INNER), jnp.float32), 0.1, 1.9),
        "w_out": bell_draw(key_of[13], (2, INNER, D), INNER ** -0.5, 0.15625),
    }


EPS_TOKEN = 1e-06
EPS_HEAD = 1e-05

def time_condition(timestep, w_time):
    half_freq = w_time.shape[0] // 2
    ladder = jnp.arange(half_freq).astype(jnp.float32)
    frequency = jnp.exp(-math.log(10000.0) * ladder / half_freq)
    angles = timestep.astype(jnp.float32)[:, None] * frequency[None, :]
    feature = jnp.concatenate([jnp.cos(angles), jnp.sin(angles)], axis=1)
    feature = jax.nn.silu(feature).astype(jnp.bfloat16)
    return jnp.dot(feature, w_time, preferred_element_type=jnp.float32)[0]

def modulate(sequence, condition, layer_index):
    model_width = sequence.shape[-1]
    values = sequence.astype(jnp.float32)
    scaled = values * lax.rsqrt(lax.optimization_barrier(jnp.mean(values * values, axis=-1, keepdims=True)) + EPS_TOKEN)
    factor = condition[2 * layer_index * model_width:(2 * layer_index + 1) * model_width]
    offset = condition[(2 * layer_index + 1) * model_width:(2 * layer_index + 2) * model_width]
    return (scaled * (1.0 + factor) + offset).astype(jnp.bfloat16)

def block_terms(x_heads, b_rows, c_rows, step_size, rates):
    high = lax.Precision.HIGHEST
    cumulative = jnp.cumsum(step_size * rates, axis=1)
    cum_heads = jnp.swapaxes(cumulative, 1, 2)
    step_heads = jnp.swapaxes(step_size, 1, 2)
    scores = jnp.einsum('ntk,nsk->nts', c_rows.astype(jnp.float32), b_rows.astype(jnp.float32), precision=high)
    length = step_size.shape[1]
    lower_mask = jnp.arange(length)[:, None] >= jnp.arange(length)[None, :]
    log_gap = cum_heads[:, :, :, None] - cum_heads[:, :, None, :]
    decay_factor = jnp.exp(jnp.where(lower_mask, log_gap, -jnp.inf))
    mixing = (scores[:, None] * decay_factor * step_heads[:, :, None, :]).astype(jnp.bfloat16)
    inside = jnp.einsum('nhts,nshp->nthp', mixing.astype(jnp.float32), x_heads.astype(jnp.float32), precision=high)
    to_end = jnp.exp(cum_heads[:, :, -1:] - cum_heads) * step_heads
    weighted = (x_heads.astype(jnp.float32) * jnp.swapaxes(to_end, 1, 2)[..., None]).astype(jnp.bfloat16)
    block_state = jnp.einsum('nshp,nsk->nhpk', weighted.astype(jnp.float32), b_rows.astype(jnp.float32), precision=high)
    return (inside, block_state, cumulative, cum_heads[:, :, -1])

def run_layer(sequence, condition, params, layer_index):
    w_in, w_dt, conv_w, conv_b, dt_bias, a_log, d_skip, out_gain, w_out = params
    high = lax.Precision.HIGHEST
    model_width = sequence.shape[1]
    rates = -jnp.exp(a_log[layer_index])
    blocks = sequence.reshape(-1, GROUP, model_width)

    def one_block(carried_in, block_x):
        entering, conv_tail = carried_in
        normed = modulate(block_x, condition, layer_index)
        projected = jnp.dot(normed, w_in[layer_index], preferred_element_type=jnp.float32)
        raw_step = jnp.dot(normed, w_dt[layer_index], preferred_element_type=jnp.float32)
        step_size = jax.nn.softplus(raw_step + dt_bias[layer_index])
        gate_z = projected[:, :INNER]
        conv_in = projected[:, INNER:]
        padded = jnp.concatenate([conv_tail, conv_in], axis=0)
        conved = conv_b[layer_index]
        for tap_index in range(CONV):
            conved = conved + conv_w[layer_index, tap_index] * padded[tap_index:tap_index + GROUP]
        conved = jax.nn.silu(conved).astype(jnp.bfloat16)
        x_heads = conved[:, :INNER].reshape(GROUP, HEADS, HDIM)
        b_rows = conved[:, INNER:INNER + STATE]
        c_rows = conved[:, INNER + STATE:]
        inside, block_state, cumulative, decay_total = block_terms(x_heads[None], b_rows[None], c_rows[None], step_size[None], rates)
        carried_part = jnp.exp(cumulative[0])[:, :, None] * jnp.einsum('ck,hpk->chp', c_rows.astype(jnp.float32), entering, precision=high)
        ssd_out = inside[0] + carried_part + d_skip[layer_index][None, :, None] * x_heads.astype(jnp.float32)
        gated = ssd_out * jax.nn.silu(gate_z).reshape(GROUP, HEADS, HDIM)
        gated = gated * lax.rsqrt(lax.optimization_barrier(jnp.mean(gated * gated, axis=-1, keepdims=True)) + EPS_HEAD)
        gated = (gated * out_gain[layer_index].reshape(HEADS, HDIM)).astype(jnp.bfloat16).reshape(GROUP, INNER)
        layer_out = (block_x.astype(jnp.float32) + jnp.dot(gated, w_out[layer_index], preferred_element_type=jnp.float32)).astype(jnp.bfloat16)
        next_enter = jnp.exp(decay_total[0])[:, None, None] * entering + block_state[0]
        return ((next_enter, padded[GROUP:]), layer_out)
    start = (jnp.zeros((HEADS, HDIM, STATE), jnp.float32), jnp.zeros((CONV - 1, CONVW), jnp.float32))
    ignored, outputs = lax.scan(one_block, start, blocks)
    return outputs.reshape(-1, model_width)

def inverse_order(order):
    return jnp.zeros_like(order).at[order].set(jnp.arange(order.shape[0]).astype(order.dtype))

def reference(tokens, timestep, col_order, row_order, w_time, w_in, w_dt, conv_w, conv_b, dt_bias, a_log, d_skip, out_gain, w_out):
    params = (w_in, w_dt, conv_w, conv_b, dt_bias, a_log, d_skip, out_gain, w_out)
    condition = time_condition(timestep, w_time)
    frames, height, breadth, model_width = tokens.shape
    row_odd = (jnp.arange(height) % 2 == 1)[None, :, None, None]
    gathered = jnp.take(tokens, col_order, axis=2)
    seq_first = jnp.where(row_odd, jnp.flip(gathered, axis=2), gathered).reshape(-1, model_width)
    out_first = run_layer(seq_first, condition, params, 0).reshape(frames, height, breadth, model_width)
    out_first = jnp.where(row_odd, jnp.flip(out_first, axis=2), out_first)
    spatial_first = jnp.take(out_first, inverse_order(col_order), axis=2)
    columns = jnp.swapaxes(spatial_first, 1, 2)
    col_odd = (jnp.arange(breadth) % 2 == 1)[None, :, None, None]
    gathered = jnp.take(columns, row_order, axis=2)
    seq_second = jnp.where(col_odd, jnp.flip(gathered, axis=2), gathered).reshape(-1, model_width)
    out_second = run_layer(seq_second, condition, params, 1).reshape(frames, breadth, height, model_width)
    out_second = jnp.where(col_odd, jnp.flip(out_second, axis=2), out_second)
    spatial_second = jnp.take(out_second, inverse_order(row_order), axis=2)
    return jnp.swapaxes(spatial_second, 1, 2)
```

```python
import math

import jax
import jax.numpy as jnp
from jax import lax
from jax.sharding import PartitionSpec as P

HEADS = 24
HDIM = 64
STATE = 128
CONV = 4
GROUP = 256
INNER = 1536


EPS_TOKEN = 1e-06
EPS_HEAD = 1e-05


def shifted(value, axis, steps):
    count = lax.axis_size(axis)
    first, last = (max(0, -steps), min(count, count - steps))
    return lax.ppermute(value, axis, [(source, source + steps) for source in range(first, last)])


def split3(value):
    high = lax.reduce_precision(value, 8, 7)
    rest = value - high
    middle = lax.reduce_precision(rest, 8, 7)
    low = lax.reduce_precision(rest - middle, 8, 7)
    return jnp.stack([high, middle, low]).astype(jnp.bfloat16)


def join3(parts, axis):
    return jnp.sum(parts.astype(jnp.float32), axis=axis)


def exchange(states, decays, axis):
    count = states.shape[0]
    flat = states.astype(jnp.bfloat16).reshape(count, -1)
    extra = jnp.broadcast_to(split3(decays).reshape(1, -1), (count, 3 * HEADS))
    message = jnp.concatenate([flat, extra], axis=1)
    got = lax.all_to_all(message, axis, split_axis=0, concat_axis=0, tiled=True)
    size = flat.shape[1]
    return (
        got[:, :size].astype(jnp.float32).reshape(states.shape),
        join3(got[:, size:].reshape(count, 3, HEADS), 1),
    )


def ladder(states, decays):
    entering = []
    running = jnp.zeros_like(states[0])
    for position in range(states.shape[0]):
        entering.append(running)
        running = running * jnp.exp(decays[position])[:, None, None] + states[position]
    return jnp.stack(entering), running


def entering_state(decay, state):
    strips = lax.axis_size("strip")
    frames = lax.axis_size("frame")
    wide = HDIM // strips
    slices = jnp.swapaxes(state.reshape(HEADS, strips, wide, STATE), 0, 1)
    pieces, decays = exchange(slices, decay, "strip")
    inside, total = ladder(pieces, decays)
    frame_decay = jnp.sum(decays, axis=0)
    totals, frame_decays = exchange(
        jnp.broadcast_to(total[None], (frames,) + total.shape), frame_decay, "frame"
    )
    before, _ = ladder(totals, frame_decays)
    mine = lax.dynamic_index_in_dim(before, lax.axis_index("frame"), 0, keepdims=False)
    reach = jnp.cumsum(decays, axis=0) - decays
    full = inside + jnp.exp(reach)[:, :, None, None] * mine[None]
    back = lax.all_to_all(full.astype(jnp.bfloat16), "strip", split_axis=0, concat_axis=0, tiled=True)
    return jnp.swapaxes(back, 0, 1).reshape(HEADS, HDIM, STATE)


def time_condition(timestep, w_time):
    half_freq = w_time.shape[0] // 2
    ladder = jnp.arange(half_freq).astype(jnp.float32)
    frequency = jnp.exp(-math.log(10000.0) * ladder / half_freq)
    angles = timestep.astype(jnp.float32)[:, None] * frequency[None, :]
    feature = jnp.concatenate([jnp.cos(angles), jnp.sin(angles)], axis=1)
    feature = jax.nn.silu(feature).astype(jnp.bfloat16)
    return jnp.dot(feature, w_time, preferred_element_type=jnp.float32)[0]


def modulate(sequence, condition, layer_index):
    model_width = sequence.shape[-1]
    values = sequence.astype(jnp.float32)
    scaled = values * lax.rsqrt(jnp.mean(values * values, axis=-1, keepdims=True) + EPS_TOKEN)
    factor = condition[2 * layer_index * model_width : (2 * layer_index + 1) * model_width]
    offset = condition[(2 * layer_index + 1) * model_width : (2 * layer_index + 2) * model_width]
    return (scaled * (1.0 + factor) + offset).astype(jnp.bfloat16)


def project(normed, w_in, w_dt, dt_bias, layer_index):
    projected = jnp.dot(normed, w_in[layer_index], preferred_element_type=jnp.float32)
    raw_step = jnp.dot(normed, w_dt[layer_index], preferred_element_type=jnp.float32)
    return (projected, jax.nn.softplus(raw_step + dt_bias[layer_index]))


def odd_lines(line_count, first_index, rank):
    parity = (first_index + jnp.arange(line_count)) % 2 == 1
    return parity.reshape((line_count,) + (1,) * (rank - 1))


def into_order(block, order, first_index):
    gathered = jnp.take(block, order, axis=1)
    odd_mask = odd_lines(block.shape[0], first_index, block.ndim)
    return jnp.where(odd_mask, jnp.flip(gathered, axis=1), gathered)


def from_order(block, order, first_index):
    odd_mask = odd_lines(block.shape[0], first_index, block.ndim)
    unflipped = jnp.where(odd_mask, jnp.flip(block, axis=1), block)
    places = jnp.zeros_like(order).at[order].set(jnp.arange(order.shape[0]))
    return jnp.take(unflipped, places, axis=1)


def block_terms(x_heads, b_rows, c_rows, step_size, rates):
    cumulative = jnp.cumsum(step_size * rates, axis=1)
    cum_heads = jnp.swapaxes(cumulative, 1, 2)
    step_heads = jnp.swapaxes(step_size, 1, 2)
    scores = jnp.einsum("ntk,nsk->nts", c_rows, b_rows, preferred_element_type=jnp.float32)
    length = step_size.shape[1]
    lower_mask = jnp.arange(length)[:, None] >= jnp.arange(length)[None, :]
    log_gap = cum_heads[:, :, :, None] - cum_heads[:, :, None, :]
    decay_factor = jnp.exp(jnp.where(lower_mask, log_gap, -jnp.inf))
    mixing = (scores[:, None] * decay_factor * step_heads[:, :, None, :]).astype(jnp.bfloat16)
    inside = jnp.einsum("nhts,nshp->nthp", mixing, x_heads, preferred_element_type=jnp.float32)
    to_end = jnp.exp(cum_heads[:, :, -1:] - cum_heads) * step_heads
    weighted = (x_heads.astype(jnp.float32) * jnp.swapaxes(to_end, 1, 2)[..., None]).astype(
        jnp.bfloat16
    )
    block_state = jnp.einsum("nshp,nsk->nhpk", weighted, b_rows, preferred_element_type=jnp.float32)
    return (inside, block_state, cumulative, cum_heads[:, :, -1])


def mixer(seq_x, projected, step_size, params, layer_index):
    w_in, w_dt, conv_w, conv_b, dt_bias, a_log, d_skip, out_gain, w_out = params
    length = seq_x.shape[0]
    blocks = length // GROUP
    gate_z = projected[:, :INNER]
    conv_in = projected[:, INNER:]
    conv_tail = shifted(conv_in[length - (CONV - 1) :], ("frame", "strip"), 1)
    padded = jnp.concatenate([conv_tail, conv_in], axis=0)
    conved = conv_b[layer_index]
    for tap_index in range(CONV):
        conved = conved + conv_w[layer_index, tap_index] * padded[tap_index : tap_index + length]
    conved = jax.nn.silu(conved).astype(jnp.bfloat16)
    x_heads = conved[:, :INNER].reshape(blocks, GROUP, HEADS, HDIM)
    b_rows = conved[:, INNER : INNER + STATE].reshape(blocks, GROUP, STATE)
    c_rows = conved[:, INNER + STATE :].reshape(blocks, GROUP, STATE)
    rates = -jnp.exp(a_log[layer_index])
    inside, block_state, cumulative, decay_total = block_terms(
        x_heads, b_rows, c_rows, step_size.reshape(blocks, GROUP, HEADS), rates
    )

    entering = entering_state(decay_total[0], block_state[0])
    carried_part = jnp.exp(cumulative)[..., None] * jnp.einsum(
        "nck,hpk->nchp", c_rows, entering, preferred_element_type=jnp.float32
    )
    ssd_out = (
        inside
        + carried_part
        + d_skip[layer_index][None, None, :, None] * x_heads.astype(jnp.float32)
    )
    gated = ssd_out.reshape(length, HEADS, HDIM) * jax.nn.silu(gate_z).reshape(length, HEADS, HDIM)
    gated = gated * lax.rsqrt(jnp.mean(gated * gated, axis=-1, keepdims=True) + EPS_HEAD)
    gated = (
        (gated * out_gain[layer_index].reshape(HEADS, HDIM))
        .astype(jnp.bfloat16)
        .reshape(length, INNER)
    )
    return (
        seq_x.astype(jnp.float32)
        + jnp.dot(gated, w_out[layer_index], preferred_element_type=jnp.float32)
    ).astype(jnp.bfloat16)


def body(
    tokens,
    timestep,
    col_order,
    row_order,
    w_time,
    w_in,
    w_dt,
    conv_w,
    conv_b,
    dt_bias,
    a_log,
    d_skip,
    out_gain,
    w_out,
):
    params = (w_in, w_dt, conv_w, conv_b, dt_bias, a_log, d_skip, out_gain, w_out)
    condition = time_condition(timestep, w_time)
    strip_index = lax.axis_index("strip")
    strips = lax.axis_size("strip")
    frame_block = tokens[0]
    rows_here, breadth, model_width = frame_block.shape
    row_start = strip_index * rows_here
    ordered = into_order(frame_block, col_order, row_start)
    seq_first = ordered.reshape(-1, model_width)
    normed_first = modulate(seq_first, condition, 0)
    projected_first, step_first = project(normed_first, w_in, w_dt, dt_bias, 0)
    out_first = mixer(seq_first, projected_first, step_first, params, 0)
    spatial_first = from_order(
        out_first.reshape(rows_here, breadth, model_width), col_order, row_start
    )
    cols_here = breadth // strips
    split_view = spatial_first.reshape(rows_here, strips, cols_here, model_width)
    piece_rows = lax.all_to_all(split_view, "strip", split_axis=1, concat_axis=0, tiled=True)
    normed = modulate(piece_rows, condition, 1)
    projected, step_size = project(normed, w_in, w_dt, dt_bias, 1)
    col_start = strip_index * cols_here

    def to_sequence(block):
        columns_first = jnp.swapaxes(block[:, 0], 0, 1)
        arranged = into_order(columns_first, row_order, col_start)
        return arranged.reshape((-1,) + arranged.shape[2:])

    seq_second = to_sequence(piece_rows)
    out_second = mixer(seq_second, to_sequence(projected), to_sequence(step_size), params, 1)
    height = piece_rows.shape[0]
    spatial_second = from_order(
        out_second.reshape(cols_here, height, model_width), row_order, col_start
    )
    return jnp.swapaxes(spatial_second, 0, 1)[None]


def solution(mesh):
    return jax.shard_map(
        body,
        mesh=mesh,
        in_specs=(
            P("frame", "strip", None, None),
            P(),
            P(),
            P(),
            P(),
            P(),
            P(),
            P(),
            P(),
            P(),
            P(),
            P(),
            P(),
            P(),
        ),
        out_specs=P("frame", None, "strip", None),
        check_vma=False,
    )
```

```python
import functools
import math

import jax
import jax.numpy as jnp
from jax import lax
from jax.experimental import pallas as pl
from jax.experimental.pallas import tpu as pltpu
from jax.sharding import PartitionSpec as P

HEADS = 24
HDIM = 64
STATE = 128
CONV = 4
GROUP = 256
INNER = 1536
CONVW = 1792
WIDTH = 768
PAIRS = INNER // 128
LAYERS = 2
EPS_TOKEN = 1e-06
EPS_HEAD = 1e-05
MESH = pl.DeviceIdType.MESH
F32 = jnp.float32
BF16 = jnp.bfloat16


def time_condition(timestep, w_time):
    half_freq = w_time.shape[0] // 2
    ladder = jnp.arange(half_freq).astype(F32)
    frequency = jnp.exp(-math.log(10000.0) * ladder / half_freq)
    angles = timestep.astype(F32)[:, None] * frequency[None, :]
    feature = jnp.concatenate([jnp.cos(angles), jnp.sin(angles)], axis=1)
    feature = jax.nn.silu(feature).astype(BF16)
    return jnp.dot(feature, w_time, preferred_element_type=F32)[0]


def dot(a, b):
    return jnp.dot(a, b, preferred_element_type=F32)


def dot_rows(a, b):
    return lax.dot_general(a, b, (((0,), (0,)), ((), ())), preferred_element_type=F32)


def dot_lanes(a, b):
    return lax.dot_general(a, b, (((1,), (1,)), ((), ())), preferred_element_type=F32)


def split(value):
    high = value.astype(BF16).astype(F32)
    rest = value - high
    middle = rest.astype(BF16).astype(F32)
    return high, middle, rest - middle


def packed(value):
    lane = lax.broadcasted_iota(jnp.int32, value.shape, 1)
    high, middle, low = split(value)
    low = jnp.where(lane < 3 * HEADS, low, 0.0)
    return jnp.where(lane < HEADS, high, jnp.where(lane < 2 * HEADS, middle, low)).astype(BF16)


def softplus(value):
    return jnp.maximum(value, 0.0) + jnp.log1p(jnp.exp(-jnp.abs(value)))


def kernel(
    strips,
    frames,
    tokens_ref,
    perm_ref,
    cond_ref,
    w_dt_ref,
    small_ref,
    conv_w_ref,
    conv_b_ref,
    gain_ref,
    w_in_ref,
    w_out_ref,
    out_ref,
    xin,
    w_in,
    w_out,
    conv,
    halo,
    gate,
    xbc,
    ssd,
    weighted,
    cum_rows,
    step_rows,
    scores,
    spread,
    gather,
    lower,
    state_send,
    state_recv,
    decay_send,
    decay_recv,
    local,
    reach,
    reach_wide,
    total_send,
    total_recv,
    fdecay_send,
    fdecay_recv,
    back_send,
    back_recv,
    tok_send,
    load_sem,
    halo_sem,
    decay_sem,
    state_sem,
    fdecay_sem,
    total_sem,
    back_sem,
    tok_sem,
):
    me_f = lax.axis_index("frame")
    me_s = lax.axis_index("strip")
    rank = me_f * strips + me_s
    count = strips * frames
    after = lax.rem(rank + 1, count)
    before = lax.rem(rank + count - 1, count)
    next_id = (lax.div(after, strips), lax.rem(after, strips))
    prev_id = (lax.div(before, strips), lax.rem(before, strips))

    def load(source, target, slot):
        return pltpu.make_async_copy(source, target, load_sem.at[slot])

    loads = [
        load(tokens_ref, xin.at[0], 0),
        load(w_in_ref.at[0], w_in.at[0], 1),
        load(w_out_ref.at[0], w_out.at[0], 2),
        load(w_in_ref.at[1], w_in.at[1], 3),
        load(w_out_ref.at[1], w_out.at[1], 4),
    ]
    for item in loads:
        item.start()

    barrier = pltpu.get_barrier_semaphore()

    def greet_strip(k, carry):
        pl.semaphore_signal(
            barrier, inc=1, device_id=(me_f, lax.rem(me_s + k, strips)), device_id_type=MESH
        )
        return carry

    def greet_frame(k, carry):
        pl.semaphore_signal(
            barrier, inc=1, device_id=(lax.rem(me_f + k, frames), me_s), device_id_type=MESH
        )
        return carry

    lax.fori_loop(1, strips, greet_strip, 0)
    lax.fori_loop(1, frames, greet_frame, 0)
    pl.semaphore_signal(barrier, inc=1, device_id=next_id, device_id_type=MESH)
    pl.semaphore_signal(barrier, inc=1, device_id=prev_id, device_id_type=MESH)

    k_id = lax.broadcasted_iota(jnp.int32, (128, INNER), 0)
    c_head = lax.broadcasted_iota(jnp.int32, (128, INNER), 1) // HDIM
    hit = (c_head == k_id) | (c_head + HEADS == k_id) | (c_head + 2 * HEADS == k_id)
    spread[...] = jnp.where(hit, 1.0, 0.0).astype(BF16)
    r_head = lax.broadcasted_iota(jnp.int32, (INNER, 128), 0) // HDIM
    l_id = lax.broadcasted_iota(jnp.int32, (INNER, 128), 1)
    hit = (r_head == l_id) | (r_head + HEADS == l_id) | (r_head + 2 * HEADS == l_id)
    gather[...] = jnp.where(hit, 1.0, 0.0).astype(BF16)
    row_id = lax.broadcasted_iota(jnp.int32, (GROUP, GROUP), 0)
    col_id = lax.broadcasted_iota(jnp.int32, (GROUP, GROUP), 1)
    lower[...] = jnp.where(row_id >= col_id, 1.0, 0.0).astype(BF16)

    def peer_copy(source, target, sem, layer, k, axis):
        if axis == "strip":
            device = (me_f, lax.rem(me_s + k, strips))
        else:
            device = (lax.rem(me_f + k, frames), me_s)
        return pltpu.make_async_remote_copy(
            src_ref=source,
            dst_ref=target,
            send_sem=sem.at[layer, 0, k],
            recv_sem=sem.at[layer, 1, k],
            device_id=device,
            device_id_type=MESH,
        )

    def strip_copies(source_of, target, sem, layer):
        def make(k):
            return peer_copy(source_of(lax.rem(me_s + k, strips)), target, sem, layer, k, "strip")

        return make, strips

    def frame_copies(source, target, sem, layer):
        def make(k):
            return peer_copy(source, target, sem, layer, k, "frame")

        return make, frames

    def start(copies):
        make, n = copies

        def one(k, carry):
            make(k).start()
            return carry

        lax.fori_loop(1, n, one, 0)

    def wait(copies):
        make, n = copies

        def one(k, carry):
            make(k).wait()
            return carry

        lax.fori_loop(1, n, one, 0)

    def run_layer(layer, carry):
        @pl.when(layer == 0)
        def _():
            loads[0].wait()

        x_rows = xin[layer].reshape(GROUP, WIDTH)
        seq_x = dot(perm_ref[2 * layer], x_rows)
        mean = jnp.mean(seq_x * seq_x, axis=-1, keepdims=True)
        normed = seq_x * lax.rsqrt(mean + EPS_TOKEN)
        normed = normed * (1.0 + cond_ref[2 * layer]) + cond_ref[2 * layer + 1]
        normed = normed.astype(BF16)

        step = softplus(dot(normed, w_dt_ref[layer]) + small_ref[layer, 0:1, :])
        log_rate = -jnp.exp(small_ref[layer, 1:2, :]) * step
        high, middle, low = split(log_rate)
        triangle = lower[...]
        cum = (
            dot(triangle, high.astype(BF16))
            + dot(triangle, middle.astype(BF16))
            + dot(triangle, low.astype(BF16))
        )
        cum_end = cum[GROUP - 1 : GROUP, :]
        decay_send[layer] = jnp.broadcast_to(cum_end, (8, 128))
        decay_recv[layer, me_s] = jnp.broadcast_to(cum_end, (8, 128))

        @pl.when(layer == 0)
        def _():
            pl.semaphore_wait(barrier, strips + frames)

        decay_out = strip_copies(
            lambda peer: decay_send.at[layer], decay_recv.at[layer, me_s], decay_sem, layer
        )
        start(decay_out)

        @pl.when(layer == 0)
        def _():
            loads[1].wait()

        @pl.when(layer == 1)
        def _():
            loads[3].wait()

        def conv_tile(i, carry):
            at = pl.multiple_of(i * 256, 256)
            conv[pl.ds(8, GROUP), pl.ds(at, 256)] = dot(
                normed, w_in[layer, :, pl.ds(pl.multiple_of(INNER + at, 256), 256)]
            )
            return carry

        lax.fori_loop(0, CONVW // 256, conv_tile, 0)
        halo_out = pltpu.make_async_remote_copy(
            src_ref=conv.at[pl.ds(GROUP, 8)],
            dst_ref=halo.at[layer],
            send_sem=halo_sem.at[layer, 0],
            recv_sem=halo_sem.at[layer, 1],
            device_id=next_id,
            device_id_type=MESH,
        )
        halo_out.start()

        def gate_tile(i, carry):
            at = pl.multiple_of(i * 256, 256)
            value = dot(normed, w_in[layer, :, pl.ds(at, 256)])
            gate[:, pl.ds(at, 256)] = value * jax.nn.sigmoid(value)
            return carry

        lax.fori_loop(0, INNER // 256, gate_tile, 0)
        cum_rows[...] = cum.T
        step_rows[...] = step.T
        cum_packed = packed(cum)
        end_packed = packed(jnp.exp(cum_end - cum) * step)
        halo_out.wait()
        conv[pl.ds(0, 8), :] = jnp.where(rank == 0, 0.0, halo[layer])

        def conv_chunk(i, carry):
            at = pl.multiple_of(i * 128, 128)
            lanes = pl.ds(at, 128)
            value = conv_b_ref[layer, :, lanes]
            for tap in range(CONV):
                value = value + conv_w_ref[layer, tap : tap + 1, lanes] * conv[
                    pl.ds(9 - CONV + tap, GROUP), lanes
                ]
            xbc[:, lanes] = (value * jax.nn.sigmoid(value)).astype(BF16)
            return carry

        lax.fori_loop(0, CONVW // 128, conv_chunk, 0)

        b_rows = xbc[:, INNER : INNER + STATE]
        c_rows = xbc[:, INNER + STATE :]

        def state_tile(i, carry):
            lanes = pl.ds(pl.multiple_of(i * 256, 256), 256)
            wide = dot(end_packed, spread[:, lanes])
            piece = (xbc[:, lanes].astype(F32) * wide).astype(BF16)
            state = dot_rows(b_rows, piece)
            state_send[layer, :, :, lanes] = state.reshape(strips, 8, 256).astype(BF16)
            return carry

        lax.fori_loop(0, INNER // 256, state_tile, 0)
        state_recv[layer, me_s] = state_send[layer, me_s]
        state_out = strip_copies(
            lambda peer: state_send.at[layer, peer], state_recv.at[layer, me_s], state_sem, layer
        )
        start(state_out)

        scores[...] = dot_lanes(c_rows, b_rows)
        ones = jnp.ones((128, GROUP), BF16)
        lane24 = lax.broadcasted_iota(jnp.int32, (1, 128), 1)
        half = GROUP // 2
        skip_wide = dot(packed(small_ref[layer, 8:16, :]), spread[...])
        lane128 = lax.broadcasted_iota(jnp.int32, (1, 128), 1)
        first_half = jnp.where(lane128 < HDIM, 1.0, 0.0).astype(BF16)
        second_half = jnp.where(lane128 < HDIM, 0.0, 1.0).astype(BF16)
        reach_wide[pl.ds(0, 8), :] = skip_wide

        def mix_pair(p, carry):
            lanes = pl.ds(pl.multiple_of(p * 128, 128), 128)
            x_pair = xbc[:, lanes]
            sides = (x_pair * first_half, x_pair * second_half)
            skip = reach_wide[0:1, lanes]
            top = skip * x_pair[:half].astype(F32)
            bottom = skip * x_pair[half:].astype(F32)
            for side in range(2):
                head = 2 * p + side
                mine = (lane24 == head) | (lane24 == head + HEADS) | (lane24 == head + 2 * HEADS)
                mask = jnp.where(mine, 1.0, 0.0).astype(BF16)
                column = dot(cum_packed * mask, ones)
                row = cum_rows[pl.ds(head, 1), :]
                row_step = step_rows[pl.ds(head, 1), :]
                gap = column[:half, :half] - row[:, :half]
                near = lower_mask_top
                decay = jnp.exp(jnp.where(near, gap, -jnp.inf))
                mixing = (scores[:half, :half] * decay * row_step[:, :half]).astype(BF16)
                top = top + dot(mixing, sides[side][:half])
                gap = column[half:, :] - row
                decay = jnp.exp(jnp.where(lower_mask_bottom, gap, -jnp.inf))
                mixing = (scores[half:, :] * decay * row_step).astype(BF16)
                bottom = bottom + dot(mixing, sides[side])
            ssd[pl.ds(0, half), lanes] = top
            ssd[pl.ds(half, half), lanes] = bottom
            return carry

        t_top = lax.broadcasted_iota(jnp.int32, (half, half), 0)
        s_top = lax.broadcasted_iota(jnp.int32, (half, half), 1)
        lower_mask_top = t_top >= s_top
        t_bottom = lax.broadcasted_iota(jnp.int32, (half, GROUP), 0) + half
        s_bottom = lax.broadcasted_iota(jnp.int32, (half, GROUP), 1)
        lower_mask_bottom = t_bottom >= s_bottom
        lax.fori_loop(0, PAIRS, mix_pair, 0)

        wait(decay_out)

        def reach_step(j, running):
            reach[j] = running
            return running + decay_recv[layer, j]

        frame_decay = lax.fori_loop(0, strips, reach_step, jnp.zeros((8, 128), F32))
        fdecay_send[layer] = frame_decay
        fdecay_recv[layer, me_f] = frame_decay
        fdecay_out = frame_copies(
            fdecay_send.at[layer], fdecay_recv.at[layer, me_f], fdecay_sem, layer
        )
        start(fdecay_out)
        own_decay = packed(jnp.exp(decay_recv[layer].reshape(strips * 8, 128)))
        decay_wide = dot(own_decay, spread[...]).reshape(strips, 8, INNER)
        reach_wide[...] = decay_wide.reshape(strips * 8, INNER)
        wait(state_out)

        def scan_step(j, running):
            local[j] = running
            rows = pl.ds(pl.multiple_of(j * 8, 8), 8)
            return running * reach_wide[rows, :] + state_recv[layer, j].astype(F32)

        total = lax.fori_loop(0, strips, scan_step, jnp.zeros((8, INNER), F32))
        total_send[layer] = total.astype(BF16)
        total_recv[layer, me_f] = total.astype(BF16)
        total_out = frame_copies(total_send.at[layer], total_recv.at[layer, me_f], total_sem, layer)
        start(total_out)
        reach_wide[...] = dot(packed(jnp.exp(reach[...].reshape(strips * 8, 128))), spread[...])
        wait(fdecay_out)
        fdecay_wide = dot(
            packed(jnp.exp(fdecay_recv[layer].reshape(frames * 8, 128))), spread[...]
        )
        wait(total_out)
        entering = jnp.zeros((8, INNER), F32)
        for g in range(frames - 1):
            longer = entering * fdecay_wide[8 * g : 8 * g + 8, :] + total_recv[layer, g].astype(F32)
            entering = jnp.where(g < me_f, longer, entering)

        def back_step(j, carry):
            rows = pl.ds(pl.multiple_of(j * 8, 8), 8)
            back_send[layer, j] = (local[j] + reach_wide[rows, :] * entering).astype(BF16)
            return carry

        lax.fori_loop(0, strips, back_step, 0)
        back_recv[layer, me_s] = back_send[layer, me_s]
        back_out = strip_copies(
            lambda peer: back_send.at[layer, peer], back_recv.at[layer, me_s], back_sem, layer
        )
        start(back_out)
        grow_packed = packed(jnp.exp(cum))
        wait(back_out)

        def gate_pair(p, squares):
            lanes = pl.ds(pl.multiple_of(p * 128, 128), 128)
            state = back_recv[layer, :, :, lanes].astype(F32).reshape(STATE, 128).astype(BF16)
            carried = dot(c_rows, state) * dot(grow_packed, spread[:, lanes])
            value = (ssd[:, lanes] + carried) * gate[:, lanes]
            ssd[:, lanes] = value
            square = value * value
            top = square.astype(BF16)
            rest = (square - top.astype(F32)).astype(BF16)
            sums = gather[pl.ds(pl.multiple_of(p * 128, 128), 128), :]
            return squares + dot(top, sums) + dot(rest, sums)

        squares = lax.fori_loop(0, PAIRS, gate_pair, jnp.zeros((GROUP, 128), F32))
        scale_packed = packed(lax.rsqrt(squares * (1.0 / HDIM) + EPS_HEAD))

        def norm_pair(p, carry):
            lanes = pl.ds(pl.multiple_of(p * 128, 128), 128)
            wide = dot(scale_packed, spread[:, lanes])
            value = ssd[:, lanes] * wide * gain_ref[layer, :, lanes]
            weighted[:, lanes] = value.astype(BF16)
            return carry

        lax.fori_loop(0, PAIRS, norm_pair, 0)

        @pl.when(layer == 0)
        def _():
            loads[2].wait()

        @pl.when(layer == 1)
        def _():
            loads[4].wait()

        layer_out = (seq_x + dot(weighted[...], w_out[layer])).astype(BF16)
        placed = dot(perm_ref[2 * layer + 1], layer_out).astype(BF16)

        @pl.when(layer == 0)
        def _():
            tok_send[...] = placed.reshape(strips, 16, WIDTH)
            xin[1, me_s] = tok_send[me_s]
            tok_out = strip_copies(lambda peer: tok_send.at[peer], xin.at[1, me_s], tok_sem, 0)
            start(tok_out)
            wait(tok_out)

        @pl.when(layer == 1)
        def _():
            out_ref[...] = placed

        return carry

    lax.fori_loop(0, LAYERS, run_layer, 0)


def one_hot(targets, size):
    return targets[:, :, None] == jnp.arange(size)[None, None, :]


def permutations(col_order, row_order):
    cols = jnp.stack([col_order, jnp.flip(col_order)])
    half = jnp.arange(2)[:, None]
    source_first = (half * 128 + cols).reshape(-1)
    place_first = ((cols // 8) * 16 + half * 8 + cols % 8).reshape(-1)
    rows = jnp.stack([row_order, jnp.flip(row_order)] * 4)
    col = jnp.arange(8)[:, None]
    source_second = (rows // 2 * 16 + rows % 2 * 8 + col).reshape(-1)
    place_second = (rows * 8 + col).reshape(-1)
    spots = jnp.arange(GROUP)
    return jnp.stack(
        [
            source_first[:, None] == spots[None, :],
            spots[:, None] == place_first[None, :],
            source_second[:, None] == spots[None, :],
            spots[:, None] == place_second[None, :],
        ]
    ).astype(BF16)


def thrice(value):
    padding = jnp.zeros(value.shape[:-1] + (128 - 3 * HEADS,), value.dtype)
    return jnp.concatenate([value, value, value, padding], axis=-1)


def body(
    strips,
    frames,
    tokens,
    timestep,
    col_order,
    row_order,
    w_time,
    w_in,
    w_dt,
    conv_w,
    conv_b,
    dt_bias,
    a_log,
    d_skip,
    out_gain,
    w_out,
):
    condition = time_condition(timestep, w_time).reshape(4, 1, WIDTH)
    small = jnp.concatenate(
        [
            thrice(dt_bias)[:, None],
            thrice(a_log)[:, None],
            jnp.zeros((LAYERS, 6, 128), F32),
            jnp.broadcast_to(thrice(d_skip)[:, None], (LAYERS, 8, 128)),
        ],
        axis=1,
    )
    vmem = pl.BlockSpec(memory_space=pltpu.VMEM)
    anywhere = pl.BlockSpec(memory_space=pl.ANY)
    dma = pltpu.SemaphoreType.DMA
    call = pl.pallas_call(
        functools.partial(kernel, strips, frames),
        out_shape=jax.ShapeDtypeStruct((GROUP, WIDTH), BF16),
        in_specs=[anywhere] + [vmem] * 7 + [anywhere] * 2,
        out_specs=vmem,
        scratch_shapes=[
            pltpu.VMEM((2, strips, 16, WIDTH), BF16),
            pltpu.VMEM((2, WIDTH, INNER + CONVW), BF16),
            pltpu.VMEM((2, INNER, WIDTH), BF16),
            pltpu.VMEM((GROUP + 8, CONVW), F32),
            pltpu.VMEM((2, 8, CONVW), F32),
            pltpu.VMEM((GROUP, INNER), F32),
            pltpu.VMEM((GROUP, CONVW), BF16),
            pltpu.VMEM((GROUP, INNER), F32),
            pltpu.VMEM((GROUP, INNER), BF16),
            pltpu.VMEM((128, GROUP), F32),
            pltpu.VMEM((128, GROUP), F32),
            pltpu.VMEM((GROUP, GROUP), F32),
            pltpu.VMEM((128, INNER), BF16),
            pltpu.VMEM((INNER, 128), BF16),
            pltpu.VMEM((GROUP, GROUP), BF16),
            pltpu.VMEM((2, strips, 8, INNER), BF16),
            pltpu.VMEM((2, strips, 8, INNER), BF16),
            pltpu.VMEM((2, 8, 128), F32),
            pltpu.VMEM((2, strips, 8, 128), F32),
            pltpu.VMEM((strips, 8, INNER), F32),
            pltpu.VMEM((strips, 8, 128), F32),
            pltpu.VMEM((strips * 8, INNER), F32),
            pltpu.VMEM((2, 8, INNER), BF16),
            pltpu.VMEM((2, frames, 8, INNER), BF16),
            pltpu.VMEM((2, 8, 128), F32),
            pltpu.VMEM((2, frames, 8, 128), F32),
            pltpu.VMEM((2, strips, 8, INNER), BF16),
            pltpu.VMEM((2, strips, 8, INNER), BF16),
            pltpu.VMEM((strips, 16, WIDTH), BF16),
            dma((5,)),
            dma((2, 2)),
            dma((2, 2, strips)),
            dma((2, 2, strips)),
            dma((2, 2, frames)),
            dma((2, 2, frames)),
            dma((2, 2, strips)),
            dma((1, 2, strips)),
        ],
        compiler_params=pltpu.CompilerParams(
            collective_id=0, has_side_effects=True, vmem_limit_bytes=60 * 1024 * 1024
        ),
    )
    out = call(
        tokens.reshape(strips, 16, WIDTH),
        permutations(col_order, row_order),
        condition,
        thrice(w_dt),
        small,
        conv_w,
        conv_b[:, None],
        out_gain[:, None],
        w_in,
        w_out,
    )
    return out.reshape(1, 32, 8, WIDTH)


def solution(mesh):
    strips, frames = mesh.shape["strip"], mesh.shape["frame"]
    return jax.shard_map(
        functools.partial(body, strips, frames),
        mesh=mesh,
        in_specs=(P("frame", "strip", None, None),) + (P(),) * 13,
        out_specs=P("frame", None, "strip", None),
        check_vma=False,
    )
```

```python
import functools
import math

import jax
import jax.numpy as jnp
from jax import lax
from jax.experimental import pallas as pl
from jax.experimental.pallas import tpu as pltpu
from jax.sharding import PartitionSpec as P

HEADS = 24
HDIM = 64
STATE = 128
CONV = 4
GROUP = 256
INNER = 1536
CONVW = 1792
WIDTH = 768
LAYERS = 2
SUB = 128
LOG2E = math.log2(math.e)
EPS_TOKEN = 1e-06
EPS_HEAD = 1e-05
MESH = pl.DeviceIdType.MESH
F32 = jnp.float32
BF16 = jnp.bfloat16


def dot(a, b):
    return jnp.dot(a, b, preferred_element_type=F32)


def dot_rows(a, b):
    return lax.dot_general(a, b, (((0,), (0,)), ((), ())), preferred_element_type=F32)


def dot_lanes(a, b):
    return lax.dot_general(a, b, (((1,), (1,)), ((), ())), preferred_element_type=F32)


def split(value):
    high = value.astype(BF16).astype(F32)
    rest = value - high
    middle = rest.astype(BF16).astype(F32)
    return high, middle, rest - middle


def packed(value):
    lane = lax.broadcasted_iota(jnp.int32, value.shape, 1)
    high, middle, low = split(value)
    low = jnp.where(lane < 3 * HEADS, low, 0.0)
    return jnp.where(lane < HEADS, high, jnp.where(lane < 2 * HEADS, middle, low)).astype(BF16)


def softplus(value):
    return jnp.maximum(value, 0.0) + jnp.log1p(jnp.exp(-jnp.abs(value)))


def kernel(
    strips,
    frames,
    time_ref,
    col_ref,
    row_ref,
    w_dt_ref,
    dt_bias_ref,
    a_log_ref,
    d_skip_ref,
    conv_w_ref,
    conv_b_ref,
    gain_ref,
    tokens_ref,
    w_time_ref,
    w_in_ref,
    w_out_ref,
    out_ref,
    xin,
    w_time,
    w_in,
    w_out,
    cond,
    perm,
    w_dt,
    conv,
    halo,
    gate,
    grow,
    xbc,
    ssd,
    gated,
    spread,
    block_ones,
    lower,
    half_state,
    state_send,
    state_recv,
    decay_send,
    decay_recv,
    local,
    reach,
    decay_wide,
    reach_wide,
    total_send,
    total_recv,
    fdecay_send,
    fdecay_recv,
    back_send,
    back_recv,
    tok_send,
    load_sem,
    halo_sem,
    decay_sem,
    state_sem,
    fdecay_sem,
    total_sem,
    back_sem,
    tok_sem,
):
    me_f = lax.axis_index("frame")
    me_s = lax.axis_index("strip")
    rank = me_f * strips + me_s
    count = strips * frames
    after = lax.rem(rank + 1, count)
    before = lax.rem(rank + count - 1, count)
    next_id = (lax.div(after, strips), lax.rem(after, strips))
    prev_id = (lax.div(before, strips), lax.rem(before, strips))

    def load(source, target, slot):
        return pltpu.make_async_copy(source, target, load_sem.at[slot])

    loads = [
        load(tokens_ref, xin.at[0], 0),
        load(w_in_ref.at[0], w_in.at[0], 1),
        load(w_out_ref.at[0], w_out.at[0], 2),
        load(w_in_ref.at[1], w_in.at[1], 3),
        load(w_out_ref.at[1], w_out.at[1], 4),
        load(w_time_ref, w_time, 5),
    ]
    for slot in (0, 5, 1, 2, 3, 4):
        loads[slot].start()

    barrier = pltpu.get_barrier_semaphore()

    def greet_strip(k, carry):
        pl.semaphore_signal(
            barrier, inc=1, device_id=(me_f, lax.rem(me_s + k, strips)), device_id_type=MESH
        )
        return carry

    def greet_frame(k, carry):
        pl.semaphore_signal(
            barrier, inc=1, device_id=(lax.rem(me_f + k, frames), me_s), device_id_type=MESH
        )
        return carry

    lax.fori_loop(1, strips, greet_strip, 0)
    lax.fori_loop(1, frames, greet_frame, 0)
    pl.semaphore_signal(barrier, inc=1, device_id=next_id, device_id_type=MESH)
    pl.semaphore_signal(barrier, inc=1, device_id=prev_id, device_id_type=MESH)

    def iota(shape, axis):
        return lax.broadcasted_iota(jnp.int32, shape, axis)

    def flag(hit):
        return jnp.where(hit, 1.0, 0.0).astype(BF16)

    spot = iota((128, GROUP), 1)
    pick = iota((128, GROUP), 0)
    turn = lax.shift_right_logical(spot, 7)
    step_in = spot & 127
    table = flag(pick == jnp.where(turn == 0, step_in, 127 - step_in))
    order = jnp.broadcast_to(col_ref[...].astype(F32), (8, 128)).astype(BF16)
    col = dot(order, table)[0:1].astype(jnp.int32)
    half = lax.shift_right_logical(spot[0:1], 7)
    source_first = half * 128 + col
    place_first = lax.shift_right_logical(col, 3) * 16 + half * 8 + (col & 7)
    spot = iota((32, GROUP), 1)
    pick = iota((32, GROUP), 0)
    turn = lax.shift_right_logical(spot, 5) & 1
    step_in = spot & 31
    table = flag(pick == jnp.where(turn == 0, step_in, 31 - step_in))
    order = jnp.broadcast_to(row_ref[...].astype(F32), (8, 32)).astype(BF16)
    row = dot(order, table)[0:1].astype(jnp.int32)
    column = lax.shift_right_logical(spot[0:1], 5)
    source_second = lax.shift_right_logical(row, 1) * 16 + (row & 1) * 8 + column
    place_second = row * 8 + column
    spots = iota((GROUP, GROUP), 0)
    for slot, target in enumerate((source_first, place_first, source_second, place_second)):
        perm[slot] = flag(spots == target)

    ladder = iota((8, 128), 1).astype(F32)
    angles = time_ref[0].astype(F32) * jnp.exp(-math.log(10000.0) * ladder / 128.0)
    waves = (jnp.cos(angles), jnp.sin(angles))
    feature = [(wave * jax.nn.sigmoid(wave)).astype(BF16) for wave in waves]

    k_id = iota((128, INNER), 0)
    c_head = lax.shift_right_logical(iota((128, INNER), 1), 6)
    spread[...] = flag(
        (c_head == k_id) | (c_head + HEADS == k_id) | (c_head + 2 * HEADS == k_id)
    )
    row_id = iota((GROUP, GROUP), 0)
    col_id = iota((GROUP, GROUP), 1)
    block_ones[...] = flag(
        lax.shift_right_logical(row_id, 6) == lax.shift_right_logical(col_id, 6)
    )
    lower[...] = flag(
        (row_id >= col_id)
        & (lax.shift_right_logical(row_id, 7) == lax.shift_right_logical(col_id, 7))
    )
    r_id = iota((HEADS, 128), 0)
    l_id = iota((HEADS, 128), 1)
    thrice = flag((l_id == r_id) | (l_id == r_id + HEADS) | (l_id == r_id + 2 * HEADS))
    for slot in range(LAYERS):
        w_dt[slot] = dot(w_dt_ref[slot], thrice).astype(BF16)

    def repeated(value):
        high, middle, low = split(value)
        return (
            dot(high.astype(BF16), thrice)
            + dot(middle.astype(BF16), thrice)
            + dot(low.astype(BF16), thrice)
        )

    dt_bias = repeated(dt_bias_ref[...])
    rates = -LOG2E * jnp.exp(repeated(a_log_ref[...]))
    d_skip = repeated(d_skip_ref[...])
    loads[5].wait()
    for slot in range(2 * LAYERS):
        lanes = pl.ds(slot * WIDTH, WIDTH)
        cond[slot] = dot(feature[0], w_time[:128, lanes]) + dot(feature[1], w_time[128:, lanes])

    def peer_copy(source, target, sem, layer, k, axis):
        if axis == "strip":
            device = (me_f, lax.rem(me_s + k, strips))
        else:
            device = (lax.rem(me_f + k, frames), me_s)
        return pltpu.make_async_remote_copy(
            src_ref=source,
            dst_ref=target,
            send_sem=sem.at[layer, 0, k],
            recv_sem=sem.at[layer, 1, k],
            device_id=device,
            device_id_type=MESH,
        )

    def strip_copies(source_of, target, sem, layer):
        def make(k):
            return peer_copy(source_of(lax.rem(me_s + k, strips)), target, sem, layer, k, "strip")

        return make, strips

    def frame_copies(source, target, sem, layer):
        def make(k):
            return peer_copy(source, target, sem, layer, k, "frame")

        return make, frames

    def start(copies):
        make, n = copies

        def one(k, carry):
            make(k).start()
            return carry

        lax.fori_loop(1, n, one, 0)

    def wait(copies):
        make, n = copies

        def one(k, carry):
            make(k).wait()
            return carry

        lax.fori_loop(1, n, one, 0)

    def wait_load(layer, slots):
        for number, slot in enumerate(slots):

            @pl.when(layer == number)
            def _(slot=slot):
                loads[slot].wait()

    def run_layer(layer, carry):
        def own(pair):
            return jnp.where(layer == 0, pair[0:1], pair[1:2])

        @pl.when(layer == 0)
        def _():
            loads[0].wait()

        seq_x = dot_rows(perm[2 * layer], xin[layer].reshape(GROUP, WIDTH))
        mean = jnp.mean(seq_x * seq_x, axis=-1, keepdims=True)
        normed = seq_x * lax.rsqrt(mean + EPS_TOKEN)
        normed = normed * (1.0 + cond[2 * layer, 0:1, :]) + cond[2 * layer + 1, 0:1, :]
        normed = normed.astype(BF16)

        wait_load(layer, (1, 3))
        for at in range(0, CONVW, 256):
            conv[pl.ds(8, GROUP), pl.ds(at, 256)] = dot(
                normed, w_in[layer, :, pl.ds(INNER + at, 256)]
            )

        @pl.when(layer == 0)
        def _():
            pl.semaphore_wait(barrier, strips + frames)

        halo_out = pltpu.make_async_remote_copy(
            src_ref=conv.at[pl.ds(GROUP, 8)],
            dst_ref=halo.at[layer],
            send_sem=halo_sem.at[layer, 0],
            recv_sem=halo_sem.at[layer, 1],
            device_id=next_id,
            device_id_type=MESH,
        )
        halo_out.start()

        step = softplus(dot(normed, w_dt[layer]) + own(dt_bias))
        high, middle, low = split(own(rates) * step)
        triangle = lower[...]
        cum = (
            dot(triangle, high.astype(BF16))
            + dot(triangle, middle.astype(BF16))
            + dot(triangle, low.astype(BF16))
        )
        ends = (cum[SUB - 1 : SUB, :], cum[GROUP - 1 : GROUP, :])
        cum_end = jnp.broadcast_to(ends[0] + ends[1], (8, 128))
        decay_send[layer] = cum_end
        decay_recv[layer, me_s] = cum_end
        decay_out = strip_copies(
            lambda peer: decay_send.at[layer], decay_recv.at[layer, me_s], decay_sem, layer
        )
        start(decay_out)
        sub_id = iota((GROUP, 128), 0)
        to_end = jnp.where(sub_id < SUB, ends[0], ends[1]) - cum
        end_packed = packed(jnp.exp2(to_end) * step)
        grow_packed = packed(jnp.exp2(cum))
        rows = (cum - LOG2E * jnp.log(step)).T
        heads_in = jnp.concatenate(
            [
                jnp.broadcast_to(own(d_skip), (8, 128)),
                jnp.broadcast_to(jnp.exp2(ends[0]), (8, 128)),
                jnp.broadcast_to(jnp.exp2(ends[1]), (8, 128)),
            ],
            axis=0,
        )
        heads_wide = dot(packed(heads_in), spread[...])
        skip_wide = heads_wide[0:1]
        shrink_first = heads_wide[8:9]
        shrink_second = heads_wide[16:17]
        halo_out.wait()
        conv[pl.ds(0, 8), :] = jnp.where(rank == 0, 0.0, halo[layer])

        for at in range(0, CONVW, 128):
            lanes = pl.ds(at, 128)
            value = own(conv_b_ref[:, lanes])
            for tap in range(CONV):
                value = value + conv_w_ref[layer, tap : tap + 1, lanes] * conv[
                    pl.ds(9 - CONV + tap, GROUP), lanes
                ]
            xbc[:, lanes] = (value * jax.nn.sigmoid(value)).astype(BF16)

        b_rows = xbc[:, INNER : INNER + STATE]
        c_rows = xbc[:, INNER + STATE :]
        for at in range(0, INNER, 256):
            lanes = pl.ds(at, 256)
            wide = dot(end_packed, spread[:, lanes])
            piece = (xbc[:, lanes].astype(F32) * wide).astype(BF16)
            first = dot_rows(b_rows[:SUB], piece[:SUB])
            half_state[:, lanes] = first
            state = first * shrink_second[:, at : at + 256] + dot_rows(b_rows[SUB:], piece[SUB:])
            state_send[layer, :, :, lanes] = state.reshape(strips, 8, 256).astype(BF16)
        state_recv[layer, me_s] = state_send[layer, me_s]
        state_out = strip_copies(
            lambda peer: state_send.at[layer, peer], state_recv.at[layer, me_s], state_sem, layer
        )
        start(state_out)

        near = iota((SUB, SUB), 0) >= iota((SUB, SUB), 1)
        scores = [dot_lanes(c_rows[at : at + SUB], b_rows[at : at + SUB]) for at in (0, SUB)]
        lane = iota((1, 128), 1)
        sides = (flag(lane < HDIM), flag(lane >= HDIM))

        def mix(pairs):
            for pair in pairs:
                lanes = pl.ds(pair * 128, 128)
                for block in range(2):
                    at = block * SUB
                    x_pair = xbc[pl.ds(at, SUB), lanes]
                    mixing = []
                    for side in range(2):
                        head = 2 * pair + side
                        gap = cum[at : at + SUB, head : head + 1] - rows[
                            head : head + 1, at : at + SUB
                        ]
                        decay = jnp.exp2(jnp.where(near, gap, -jnp.inf))
                        mixing.append((scores[block] * decay).astype(BF16))
                    inside = dot(
                        jnp.concatenate(mixing, axis=1),
                        jnp.concatenate([x_pair * sides[0], x_pair * sides[1]], axis=0),
                    )
                    skip = skip_wide[:, pair * 128 : pair * 128 + 128] * x_pair.astype(F32)
                    ssd[pl.ds(at, SUB), lanes] = inside + skip

        for at in range(0, INNER, 256):
            value = dot(normed, w_in[layer, :, pl.ds(at, 256)])
            gate[:, pl.ds(at, 256)] = value * jax.nn.sigmoid(value)
        mix(range(0, 4))

        wait(decay_out)
        running = jnp.zeros((8, 128), F32)
        for j in range(strips):
            reach[j] = running
            running = running + decay_recv[layer, j]
        fdecay_send[layer] = running
        fdecay_recv[layer, me_f] = running
        fdecay_out = frame_copies(
            fdecay_send.at[layer], fdecay_recv.at[layer, me_f], fdecay_sem, layer
        )
        start(fdecay_out)
        own_decay = packed(jnp.exp2(decay_recv[layer].reshape(strips * 8, 128)))
        decay_wide[...] = dot(own_decay, spread[...]).reshape(strips, 8, INNER)
        wait(state_out)
        running = jnp.zeros((8, INNER), F32)
        for j in range(strips):
            local[j] = running
            running = running * decay_wide[j] + state_recv[layer, j].astype(F32)
        total_send[layer] = running.astype(BF16)
        total_recv[layer, me_f] = running.astype(BF16)
        total_out = frame_copies(total_send.at[layer], total_recv.at[layer, me_f], total_sem, layer)
        start(total_out)
        own_reach = packed(jnp.exp2(reach[...].reshape(strips * 8, 128)))
        reach_wide[...] = dot(own_reach, spread[...]).reshape(strips, 8, INNER)
        mix(range(4, 8))
        wait(fdecay_out)
        fdecay_wide = dot(
            packed(jnp.exp2(fdecay_recv[layer].reshape(frames * 8, 128))), spread[...]
        )
        wait(total_out)
        entering = jnp.zeros((8, INNER), F32)
        for g in range(frames - 1):
            longer = entering * fdecay_wide[8 * g : 8 * g + 8, :] + total_recv[layer, g].astype(F32)
            entering = jnp.where(g < me_f, longer, entering)
        for j in range(strips):
            back_send[layer, j] = (local[j] + reach_wide[j] * entering).astype(BF16)
        back_recv[layer, me_s] = back_send[layer, me_s]
        back_out = strip_copies(
            lambda peer: back_send.at[layer, peer], back_recv.at[layer, me_s], back_sem, layer
        )
        start(back_out)
        mix(range(8, 12))
        for at in range(0, INNER, 256):
            lanes = pl.ds(at, 256)
            wide = dot(grow_packed, spread[:, lanes])
            ssd[:, lanes] = ssd[:, lanes] * gate[:, lanes]
            grow[:, lanes] = wide * gate[:, lanes]
        wait(back_out)

        for at in range(0, INNER, 256):
            lanes = pl.ds(at, 256)
            state = back_recv[layer, :, :, lanes].astype(F32).reshape(STATE, 256)
            later = state * shrink_first[:, at : at + 256] + half_state[:, lanes]
            carried = jnp.concatenate(
                [dot(c_rows[:SUB], state.astype(BF16)), dot(c_rows[SUB:], later.astype(BF16))],
                axis=0,
            )
            value = ssd[:, lanes] + carried * grow[:, lanes]
            square = value * value
            top = square.astype(BF16)
            rest = (square - top.astype(F32)).astype(BF16)
            sums = dot(top, block_ones[...]) + dot(rest, block_ones[...])
            scale = lax.rsqrt(sums * (1.0 / HDIM) + EPS_HEAD)
            gated[:, lanes] = (value * scale * own(gain_ref[:, lanes])).astype(BF16)

        wait_load(layer, (2, 4))
        layer_out = (seq_x + dot(gated[...], w_out[layer])).astype(BF16)
        placed = dot(perm[2 * layer + 1], layer_out).astype(BF16)

        @pl.when(layer == 0)
        def _():
            tok_send[...] = placed.reshape(strips, 16, WIDTH)
            xin[1, me_s] = tok_send[me_s]
            tok_out = strip_copies(lambda peer: tok_send.at[peer], xin.at[1, me_s], tok_sem, 0)
            start(tok_out)
            wait(tok_out)

        @pl.when(layer == 1)
        def _():
            out_ref[...] = placed

        return carry

    lax.fori_loop(0, LAYERS, run_layer, 0)


def body(
    strips,
    frames,
    tokens,
    timestep,
    col_order,
    row_order,
    w_time,
    w_in,
    w_dt,
    conv_w,
    conv_b,
    dt_bias,
    a_log,
    d_skip,
    out_gain,
    w_out,
):
    vmem = pl.BlockSpec(memory_space=pltpu.VMEM)
    smem = pl.BlockSpec(memory_space=pltpu.SMEM)
    anywhere = pl.BlockSpec(memory_space=pl.ANY)
    dma = pltpu.SemaphoreType.DMA
    call = pl.pallas_call(
        functools.partial(kernel, strips, frames),
        out_shape=jax.ShapeDtypeStruct((GROUP, WIDTH), BF16),
        in_specs=[smem] + [vmem] * 9 + [anywhere] * 4,
        out_specs=vmem,
        scratch_shapes=[
            pltpu.VMEM((2, strips, 16, WIDTH), BF16),
            pltpu.VMEM((256, 2 * LAYERS * WIDTH), BF16),
            pltpu.VMEM((2, WIDTH, INNER + CONVW), BF16),
            pltpu.VMEM((2, INNER, WIDTH), BF16),
            pltpu.VMEM((2 * LAYERS, 8, WIDTH), F32),
            pltpu.VMEM((2 * LAYERS, GROUP, GROUP), BF16),
            pltpu.VMEM((2, WIDTH, 128), BF16),
            pltpu.VMEM((GROUP + 8, CONVW), F32),
            pltpu.VMEM((2, 8, CONVW), F32),
            pltpu.VMEM((GROUP, INNER), F32),
            pltpu.VMEM((GROUP, INNER), F32),
            pltpu.VMEM((GROUP, CONVW), BF16),
            pltpu.VMEM((GROUP, INNER), F32),
            pltpu.VMEM((GROUP, INNER), BF16),
            pltpu.VMEM((128, INNER), BF16),
            pltpu.VMEM((GROUP, GROUP), BF16),
            pltpu.VMEM((GROUP, GROUP), BF16),
            pltpu.VMEM((STATE, INNER), F32),
            pltpu.VMEM((2, strips, 8, INNER), BF16),
            pltpu.VMEM((2, strips, 8, INNER), BF16),
            pltpu.VMEM((2, 8, 128), F32),
            pltpu.VMEM((2, strips, 8, 128), F32),
            pltpu.VMEM((strips, 8, INNER), F32),
            pltpu.VMEM((strips, 8, 128), F32),
            pltpu.VMEM((strips, 8, INNER), F32),
            pltpu.VMEM((strips, 8, INNER), F32),
            pltpu.VMEM((2, 8, INNER), BF16),
            pltpu.VMEM((2, frames, 8, INNER), BF16),
            pltpu.VMEM((2, 8, 128), F32),
            pltpu.VMEM((2, frames, 8, 128), F32),
            pltpu.VMEM((2, strips, 8, INNER), BF16),
            pltpu.VMEM((2, strips, 8, INNER), BF16),
            pltpu.VMEM((strips, 16, WIDTH), BF16),
            dma((6,)),
            dma((2, 2)),
            dma((2, 2, strips)),
            dma((2, 2, strips)),
            dma((2, 2, frames)),
            dma((2, 2, frames)),
            dma((2, 2, strips)),
            dma((1, 2, strips)),
        ],
        compiler_params=pltpu.CompilerParams(
            collective_id=0, has_side_effects=True, vmem_limit_bytes=60 * 1024 * 1024
        ),
    )
    out = call(
        timestep,
        col_order.reshape(1, 128),
        row_order.reshape(1, 32),
        w_dt,
        dt_bias,
        a_log,
        d_skip,
        conv_w,
        conv_b,
        out_gain,
        tokens.reshape(strips, 16, WIDTH),
        w_time,
        w_in,
        w_out,
    )
    return out.reshape(1, 32, 8, WIDTH)


def solution(mesh):
    strips, frames = mesh.shape["strip"], mesh.shape["frame"]
    return jax.shard_map(
        functools.partial(body, strips, frames),
        mesh=mesh,
        in_specs=(P("frame", "strip", None, None),) + (P(),) * 13,
        out_specs=P("frame", None, "strip", None),
        check_vma=False,
    )
```

```python
import functools
import math

import jax
import jax.numpy as jnp
from jax import lax
from jax.experimental import pallas as pl
from jax.experimental.pallas import tpu as pltpu
from jax.sharding import PartitionSpec as P

HEADS = 24
HDIM = 64
STATE = 128
CONV = 4
GROUP = 256
INNER = 1536
CONVW = 1792
WIDTH = 768
LAYERS = 2
SUB = 128
LOG2E = math.log2(math.e)
EPS_TOKEN = 1e-06
EPS_HEAD = 1e-05
MESH = pl.DeviceIdType.MESH
F32 = jnp.float32
BF16 = jnp.bfloat16


def dot(a, b):
    return jnp.dot(a, b, preferred_element_type=F32)


def dot_rows(a, b):
    return lax.dot_general(a, b, (((0,), (0,)), ((), ())), preferred_element_type=F32)


def dot_lanes(a, b):
    return lax.dot_general(a, b, (((1,), (1,)), ((), ())), preferred_element_type=F32)


def split(value):
    high = value.astype(BF16).astype(F32)
    rest = value - high
    middle = rest.astype(BF16).astype(F32)
    return high, middle, rest - middle


def packed(value):
    lane = lax.broadcasted_iota(jnp.int32, value.shape, 1)
    high, middle, low = split(value)
    low = jnp.where(lane < 3 * HEADS, low, 0.0)
    return jnp.where(lane < HEADS, high, jnp.where(lane < 2 * HEADS, middle, low)).astype(BF16)


def softplus(value):
    return jnp.maximum(value, 0.0) + jnp.log1p(jnp.exp(-jnp.abs(value)))


def kernel(
    strips,
    frames,
    time_ref,
    col_ref,
    row_ref,
    w_dt_ref,
    dt_bias_ref,
    a_log_ref,
    d_skip_ref,
    conv_w_ref,
    conv_b_ref,
    gain_ref,
    tokens_ref,
    w_time_ref,
    w_in_ref,
    w_out_ref,
    out_ref,
    xin,
    w_time,
    w_in,
    w_out,
    cond,
    perm,
    w_dt,
    conv,
    halo,
    gate,
    grow,
    xbc,
    ssd,
    gated,
    spread,
    block_ones,
    lower,
    half_state,
    state_send,
    state_recv,
    decay_send,
    decay_recv,
    local,
    reach,
    decay_wide,
    reach_wide,
    total_send,
    total_recv,
    fdecay_send,
    fdecay_recv,
    back_send,
    back_recv,
    tok_send,
    load_sem,
    halo_sem,
    decay_sem,
    state_sem,
    fdecay_sem,
    total_sem,
    back_sem,
    tok_sem,
):
    me_f = lax.axis_index("frame")
    me_s = lax.axis_index("strip")
    rank = me_f * strips + me_s
    count = strips * frames
    after = lax.rem(rank + 1, count)
    before = lax.rem(rank + count - 1, count)
    next_id = (lax.div(after, strips), lax.rem(after, strips))
    prev_id = (lax.div(before, strips), lax.rem(before, strips))

    def load(source, target, slot):
        return pltpu.make_async_copy(source, target, load_sem.at[slot])

    loads = [
        load(tokens_ref, xin.at[0], 0),
        load(w_in_ref.at[0], w_in.at[0], 1),
        load(w_out_ref.at[0], w_out.at[0], 2),
        load(w_in_ref.at[1], w_in.at[1], 3),
        load(w_out_ref.at[1], w_out.at[1], 4),
        load(w_time_ref, w_time, 5),
    ]
    for slot in (0, 5, 1, 2, 3, 4):
        loads[slot].start()

    barrier = pltpu.get_barrier_semaphore()

    def greet_strip(k, carry):
        pl.semaphore_signal(
            barrier, inc=1, device_id=(me_f, lax.rem(me_s + k, strips)), device_id_type=MESH
        )
        return carry

    def greet_frame(k, carry):
        pl.semaphore_signal(
            barrier, inc=1, device_id=(lax.rem(me_f + k, frames), me_s), device_id_type=MESH
        )
        return carry

    lax.fori_loop(1, strips, greet_strip, 0)
    lax.fori_loop(1, frames, greet_frame, 0)
    pl.semaphore_signal(barrier, inc=1, device_id=next_id, device_id_type=MESH)
    pl.semaphore_signal(barrier, inc=1, device_id=prev_id, device_id_type=MESH)

    def iota(shape, axis):
        return lax.broadcasted_iota(jnp.int32, shape, axis)

    def flag(hit):
        return jnp.where(hit, 1.0, 0.0).astype(BF16)

    spot = iota((128, GROUP), 1)
    pick = iota((128, GROUP), 0)
    turn = lax.shift_right_logical(spot, 7)
    step_in = spot & 127
    table = flag(pick == jnp.where(turn == 0, step_in, 127 - step_in))
    order = jnp.broadcast_to(col_ref[...].astype(F32), (8, 128)).astype(BF16)
    col = dot(order, table)[0:1].astype(jnp.int32)
    half = lax.shift_right_logical(spot[0:1], 7)
    source_first = half * 128 + col
    place_first = lax.shift_right_logical(col, 3) * 16 + half * 8 + (col & 7)
    spot = iota((32, GROUP), 1)
    pick = iota((32, GROUP), 0)
    turn = lax.shift_right_logical(spot, 5) & 1
    step_in = spot & 31
    table = flag(pick == jnp.where(turn == 0, step_in, 31 - step_in))
    order = jnp.broadcast_to(row_ref[...].astype(F32), (8, 32)).astype(BF16)
    row = dot(order, table)[0:1].astype(jnp.int32)
    column = lax.shift_right_logical(spot[0:1], 5)
    source_second = lax.shift_right_logical(row, 1) * 16 + (row & 1) * 8 + column
    place_second = row * 8 + column
    spots = iota((GROUP, GROUP), 0)
    for slot, target in enumerate((source_first, place_first, source_second, place_second)):
        perm[slot] = flag(spots == target)

    ladder = iota((8, 128), 1).astype(F32)
    angles = time_ref[0].astype(F32) * jnp.exp(-math.log(10000.0) * ladder / 128.0)
    waves = (jnp.cos(angles), jnp.sin(angles))
    feature = [(wave * jax.nn.sigmoid(wave)).astype(BF16) for wave in waves]

    k_id = iota((128, INNER), 0)
    c_head = lax.shift_right_logical(iota((128, INNER), 1), 6)
    spread[...] = flag(
        (c_head == k_id) | (c_head + HEADS == k_id) | (c_head + 2 * HEADS == k_id)
    )
    row_id = iota((GROUP, GROUP), 0)
    col_id = iota((GROUP, GROUP), 1)
    block_ones[...] = flag(
        lax.shift_right_logical(row_id, 6) == lax.shift_right_logical(col_id, 6)
    )
    lower[...] = flag(
        (row_id >= col_id)
        & (lax.shift_right_logical(row_id, 7) == lax.shift_right_logical(col_id, 7))
    )
    r_id = iota((HEADS, 128), 0)
    l_id = iota((HEADS, 128), 1)
    thrice = flag((l_id == r_id) | (l_id == r_id + HEADS) | (l_id == r_id + 2 * HEADS))
    for slot in range(LAYERS):
        w_dt[slot] = dot_rows(w_dt_ref[slot], thrice).astype(BF16)

    def repeated(value):
        high, middle, low = split(value)
        return (
            dot(high.astype(BF16), thrice)
            + dot(middle.astype(BF16), thrice)
            + dot(low.astype(BF16), thrice)
        )

    dt_bias = repeated(dt_bias_ref[...])
    rates = -LOG2E * jnp.exp(repeated(a_log_ref[...]))
    d_skip = repeated(d_skip_ref[...])
    loads[5].wait()
    for slot in range(2 * LAYERS):
        lanes = pl.ds(slot * WIDTH, WIDTH)
        cond[slot] = dot(feature[0], w_time[:128, lanes]) + dot(feature[1], w_time[128:, lanes])

    side = 4
    hops = (0, 1, 2, 1)
    spots_x = [lax.rem(lax.div(me_s, side) + step, side) for step in range(side)]
    spots_z = [lax.rem(lax.rem(me_s, side) + step, side) for step in range(side)]
    strip_peers = [
        spots_x[dx] * side + spots_z[dz]
        for dx, dz in sorted(
            [(dx, dz) for dx in range(side) for dz in range(side) if dx or dz],
            key=lambda offset: -hops[offset[0]] - hops[offset[1]],
        )
    ]
    spots_y = [lax.rem(lax.div(me_f, 2) + step, side) for step in range(side)]
    spots_c = [lax.rem(lax.rem(me_f, 2) + step, 2) for step in range(2)]
    frame_peers = [
        spots_y[dy] * 2 + spots_c[dc]
        for dy, dc in sorted(
            [(dy, dc) for dy in range(side) for dc in range(2) if dy or dc],
            key=lambda offset: -hops[offset[0]],
        )
    ]

    def peer_copy(source, target, sem, layer, k, device):
        return pltpu.make_async_remote_copy(
            src_ref=source,
            dst_ref=target,
            send_sem=sem.at[layer, 0, k],
            recv_sem=sem.at[layer, 1, k],
            device_id=device,
            device_id_type=MESH,
        )

    def strip_copies(source_of, target, sem, layer):
        return [
            peer_copy(source_of(peer), target, sem, layer, k, (me_f, peer))
            for k, peer in enumerate(strip_peers)
        ]

    def frame_copies(source, target, sem, layer):
        return [
            peer_copy(source, target, sem, layer, k, (peer, me_s))
            for k, peer in enumerate(frame_peers)
        ]

    def start(copies):
        for item in copies:
            item.start()

    def wait(copies):
        for item in copies:
            item.wait()

    def wait_load(layer, slots):
        for number, slot in enumerate(slots):

            @pl.when(layer == number)
            def _(slot=slot):
                loads[slot].wait()

    def run_layer(layer, carry):
        def own(pair):
            return jnp.where(layer == 0, pair[0:1], pair[1:2])

        @pl.when(layer == 0)
        def _():
            loads[0].wait()

        seq_x = dot_rows(perm[2 * layer], xin[layer].reshape(GROUP, WIDTH))
        mean = jnp.mean(seq_x * seq_x, axis=-1, keepdims=True)
        normed = seq_x * lax.rsqrt(mean + EPS_TOKEN)
        normed = normed * (1.0 + cond[2 * layer, 0:1, :]) + cond[2 * layer + 1, 0:1, :]
        normed = normed.astype(BF16)

        wait_load(layer, (1, 3))
        for at in range(0, CONVW, 256):
            conv[pl.ds(8, GROUP), pl.ds(at, 256)] = dot(
                normed, w_in[layer, :, pl.ds(INNER + at, 256)]
            )

        @pl.when(layer == 0)
        def _():
            pl.semaphore_wait(barrier, strips + frames)

        halo_out = pltpu.make_async_remote_copy(
            src_ref=conv.at[pl.ds(GROUP, 8)],
            dst_ref=halo.at[layer],
            send_sem=halo_sem.at[layer, 0],
            recv_sem=halo_sem.at[layer, 1],
            device_id=next_id,
            device_id_type=MESH,
        )
        halo_out.start()

        step = softplus(dot(normed, w_dt[layer]) + own(dt_bias))
        high, middle, low = split(own(rates) * step)
        triangle = lower[...]
        cum = (
            dot(triangle, high.astype(BF16))
            + dot(triangle, middle.astype(BF16))
            + dot(triangle, low.astype(BF16))
        )
        ends = (cum[SUB - 1 : SUB, :], cum[GROUP - 1 : GROUP, :])
        cum_end = jnp.broadcast_to(ends[0] + ends[1], (8, 128))
        decay_send[layer] = cum_end
        decay_recv[layer, me_s] = cum_end
        decay_out = strip_copies(
            lambda peer: decay_send.at[layer], decay_recv.at[layer, me_s], decay_sem, layer
        )
        start(decay_out)
        sub_id = iota((GROUP, 128), 0)
        to_end = jnp.where(sub_id < SUB, ends[0], ends[1]) - cum
        end_packed = packed(jnp.exp2(to_end) * step)
        grow_packed = packed(jnp.exp2(cum))
        rows = (cum - LOG2E * jnp.log(step)).T
        heads_in = jnp.concatenate(
            [
                jnp.broadcast_to(own(d_skip), (8, 128)),
                jnp.broadcast_to(jnp.exp2(ends[0]), (8, 128)),
                jnp.broadcast_to(jnp.exp2(ends[1]), (8, 128)),
            ],
            axis=0,
        )
        heads_wide = dot(packed(heads_in), spread[...])
        skip_wide = heads_wide[0:1]
        shrink_first = heads_wide[8:9]
        shrink_second = heads_wide[16:17]
        for at in range(0, INNER, 256):
            value = dot(normed, w_in[layer, :, pl.ds(at, 256)])
            gate[:, pl.ds(at, 256)] = value * jax.nn.sigmoid(value)

        def convolve(top, count):
            for at in range(0, CONVW, 128):
                lanes = pl.ds(at, 128)
                value = own(conv_b_ref[:, lanes])
                for tap in range(CONV):
                    value = value + conv_w_ref[layer, tap : tap + 1, lanes] * conv[
                        pl.ds(top + 9 - CONV + tap, count), lanes
                    ]
                xbc[pl.ds(top, count), lanes] = (value * jax.nn.sigmoid(value)).astype(BF16)

        def sub_state(top, lanes):
            b_part = xbc[pl.ds(top, SUB), INNER : INNER + STATE]
            wide = dot(end_packed[top : top + SUB], spread[:, lanes])
            piece = (xbc[pl.ds(top, SUB), lanes].astype(F32) * wide).astype(BF16)
            return dot_rows(b_part, piece)

        convolve(16, GROUP - 16)
        for at in range(0, INNER, 256):
            lanes = pl.ds(at, 256)
            grow[pl.ds(0, STATE), lanes] = sub_state(SUB, lanes)
        halo_out.wait()
        conv[pl.ds(0, 8), :] = jnp.where(rank == 0, 0.0, halo[layer])
        convolve(0, 16)

        b_rows = xbc[:, INNER : INNER + STATE]
        c_rows = xbc[:, INNER + STATE :]
        for at in range(0, INNER, 256):
            lanes = pl.ds(at, 256)
            first = sub_state(0, lanes)
            half_state[:, lanes] = first
            state = first * shrink_second[:, at : at + 256] + grow[pl.ds(0, STATE), lanes]
            state_send[layer, :, :, lanes] = state.reshape(strips, 8, 256).astype(BF16)
        state_recv[layer, me_s] = state_send[layer, me_s]
        state_out = strip_copies(
            lambda peer: state_send.at[layer, peer], state_recv.at[layer, me_s], state_sem, layer
        )
        start(state_out)

        near = iota((SUB, SUB), 0) >= iota((SUB, SUB), 1)
        scores = [dot_lanes(c_rows[at : at + SUB], b_rows[at : at + SUB]) for at in (0, SUB)]
        lane = iota((1, 128), 1)
        sides = (flag(lane < HDIM), flag(lane >= HDIM))

        def mix(pairs):
            for pair in pairs:
                lanes = pl.ds(pair * 128, 128)
                for block in range(2):
                    at = block * SUB
                    x_pair = xbc[pl.ds(at, SUB), lanes]
                    mixing = []
                    for side in range(2):
                        head = 2 * pair + side
                        gap = cum[at : at + SUB, head : head + 1] - rows[
                            head : head + 1, at : at + SUB
                        ]
                        decay = jnp.exp2(jnp.where(near, gap, -jnp.inf))
                        mixing.append((scores[block] * decay).astype(BF16))
                    inside = dot(
                        jnp.concatenate(mixing, axis=1),
                        jnp.concatenate([x_pair * sides[0], x_pair * sides[1]], axis=0),
                    )
                    skip = skip_wide[:, pair * 128 : pair * 128 + 128] * x_pair.astype(F32)
                    ssd[pl.ds(at, SUB), lanes] = inside + skip

        mix(range(0, 4))

        wait(decay_out)
        running = jnp.zeros((8, 128), F32)
        for j in range(strips):
            reach[j] = running
            running = running + decay_recv[layer, j]
        fdecay_send[layer] = running
        fdecay_recv[layer, me_f] = running
        fdecay_out = frame_copies(
            fdecay_send.at[layer], fdecay_recv.at[layer, me_f], fdecay_sem, layer
        )
        start(fdecay_out)
        own_decay = packed(jnp.exp2(decay_recv[layer].reshape(strips * 8, 128)))
        decay_wide[...] = dot(own_decay, spread[...]).reshape(strips, 8, INNER)
        wait(state_out)
        running = jnp.zeros((8, INNER), F32)
        for j in range(strips):
            local[j] = running
            running = running * decay_wide[j] + state_recv[layer, j].astype(F32)
        total_send[layer] = running.astype(BF16)
        total_recv[layer, me_f] = running.astype(BF16)
        total_out = frame_copies(total_send.at[layer], total_recv.at[layer, me_f], total_sem, layer)
        start(total_out)
        own_reach = packed(jnp.exp2(reach[...].reshape(strips * 8, 128)))
        reach_wide[...] = dot(own_reach, spread[...]).reshape(strips, 8, INNER)
        mix(range(4, 8))
        wait(fdecay_out)
        fdecay_wide = dot(
            packed(jnp.exp2(fdecay_recv[layer].reshape(frames * 8, 128))), spread[...]
        )
        wait(total_out)
        entering = jnp.zeros((8, INNER), F32)
        for g in range(frames - 1):
            longer = entering * fdecay_wide[8 * g : 8 * g + 8, :] + total_recv[layer, g].astype(F32)
            entering = jnp.where(g < me_f, longer, entering)
        for j in range(strips):
            back_send[layer, j] = (local[j] + reach_wide[j] * entering).astype(BF16)
        back_recv[layer, me_s] = back_send[layer, me_s]
        back_out = strip_copies(
            lambda peer: back_send.at[layer, peer], back_recv.at[layer, me_s], back_sem, layer
        )
        start(back_out)
        mix(range(8, 12))
        for at in range(0, INNER, 256):
            lanes = pl.ds(at, 256)
            wide = dot(grow_packed, spread[:, lanes])
            ssd[:, lanes] = ssd[:, lanes] * gate[:, lanes]
            grow[:, lanes] = wide * gate[:, lanes]
        wait(back_out)

        for at in range(0, INNER, 256):
            lanes = pl.ds(at, 256)
            state = back_recv[layer, :, :, lanes].astype(F32).reshape(STATE, 256)
            later = state * shrink_first[:, at : at + 256] + half_state[:, lanes]
            carried = jnp.concatenate(
                [dot(c_rows[:SUB], state.astype(BF16)), dot(c_rows[SUB:], later.astype(BF16))],
                axis=0,
            )
            value = ssd[:, lanes] + carried * grow[:, lanes]
            square = value * value
            top = square.astype(BF16)
            rest = (square - top.astype(F32)).astype(BF16)
            sums = dot(top, block_ones[...]) + dot(rest, block_ones[...])
            scale = lax.rsqrt(sums * (1.0 / HDIM) + EPS_HEAD)
            gated[:, lanes] = (value * scale * own(gain_ref[:, lanes])).astype(BF16)

        wait_load(layer, (2, 4))
        layer_out = (seq_x + dot(gated[...], w_out[layer])).astype(BF16)
        placed = dot(perm[2 * layer + 1], layer_out)

        @pl.when(layer == 0)
        def _():
            tok_send[...] = placed.astype(BF16).reshape(strips, 16, WIDTH)
            xin[1, me_s] = tok_send[me_s]
            tok_out = strip_copies(lambda peer: tok_send.at[peer], xin.at[1, me_s], tok_sem, 0)
            start(tok_out)
            wait(tok_out)

        @pl.when(layer == 1)
        def _():
            out_ref[...] = placed.reshape(32, 8, WIDTH).astype(BF16)

        return carry

    lax.fori_loop(0, LAYERS, run_layer, 0)


def body(
    strips,
    frames,
    tokens,
    timestep,
    col_order,
    row_order,
    w_time,
    w_in,
    w_dt,
    conv_w,
    conv_b,
    dt_bias,
    a_log,
    d_skip,
    out_gain,
    w_out,
):
    vmem = pl.BlockSpec(memory_space=pltpu.VMEM)
    smem = pl.BlockSpec(memory_space=pltpu.SMEM)
    anywhere = pl.BlockSpec(memory_space=pl.ANY)
    dma = pltpu.SemaphoreType.DMA
    call = pl.pallas_call(
        functools.partial(kernel, strips, frames),
        out_shape=jax.ShapeDtypeStruct((32, 8, WIDTH), BF16),
        in_specs=[smem] + [vmem] * 9 + [anywhere] * 4,
        out_specs=vmem,
        scratch_shapes=[
            pltpu.VMEM((2, strips, 16, WIDTH), BF16),
            pltpu.VMEM((256, 2 * LAYERS * WIDTH), BF16),
            pltpu.VMEM((2, WIDTH, INNER + CONVW), BF16),
            pltpu.VMEM((2, INNER, WIDTH), BF16),
            pltpu.VMEM((2 * LAYERS, 8, WIDTH), F32),
            pltpu.VMEM((2 * LAYERS, GROUP, GROUP), BF16),
            pltpu.VMEM((2, WIDTH, 128), BF16),
            pltpu.VMEM((GROUP + 8, CONVW), F32),
            pltpu.VMEM((2, 8, CONVW), F32),
            pltpu.VMEM((GROUP, INNER), F32),
            pltpu.VMEM((GROUP, INNER), F32),
            pltpu.VMEM((GROUP, CONVW), BF16),
            pltpu.VMEM((GROUP, INNER), F32),
            pltpu.VMEM((GROUP, INNER), BF16),
            pltpu.VMEM((128, INNER), BF16),
            pltpu.VMEM((GROUP, GROUP), BF16),
            pltpu.VMEM((GROUP, GROUP), BF16),
            pltpu.VMEM((STATE, INNER), F32),
            pltpu.VMEM((2, strips, 8, INNER), BF16),
            pltpu.VMEM((2, strips, 8, INNER), BF16),
            pltpu.VMEM((2, 8, 128), F32),
            pltpu.VMEM((2, strips, 8, 128), F32),
            pltpu.VMEM((strips, 8, INNER), F32),
            pltpu.VMEM((strips, 8, 128), F32),
            pltpu.VMEM((strips, 8, INNER), F32),
            pltpu.VMEM((strips, 8, INNER), F32),
            pltpu.VMEM((2, 8, INNER), BF16),
            pltpu.VMEM((2, frames, 8, INNER), BF16),
            pltpu.VMEM((2, 8, 128), F32),
            pltpu.VMEM((2, frames, 8, 128), F32),
            pltpu.VMEM((2, strips, 8, INNER), BF16),
            pltpu.VMEM((2, strips, 8, INNER), BF16),
            pltpu.VMEM((strips, 16, WIDTH), BF16),
            dma((6,)),
            dma((2, 2)),
            dma((2, 2, strips)),
            dma((2, 2, strips)),
            dma((2, 2, frames)),
            dma((2, 2, frames)),
            dma((2, 2, strips)),
            dma((1, 2, strips)),
        ],
        compiler_params=pltpu.CompilerParams(
            collective_id=0, has_side_effects=True, vmem_limit_bytes=60 * 1024 * 1024
        ),
    )
    out = call(
        timestep,
        col_order.reshape(1, 128),
        row_order.reshape(1, 32),
        jnp.swapaxes(w_dt, 1, 2),
        dt_bias,
        a_log,
        d_skip,
        conv_w,
        conv_b,
        out_gain,
        tokens.reshape(strips, 16, WIDTH),
        w_time,
        w_in,
        w_out,
    )
    return out.reshape(1, 32, 8, WIDTH)


def solution(mesh):
    strips, frames = mesh.shape["strip"], mesh.shape["frame"]
    return jax.shard_map(
        functools.partial(body, strips, frames),
        mesh=mesh,
        in_specs=(P("frame", "strip", None, None),) + (P(),) * 13,
        out_specs=P("frame", None, "strip", None),
        check_vma=False,
    )
```
